32 devices in a mesh: grp: 2 (over y), blk: 4 (over z), bulk: 4 (over x, core).
Axes of the slice: x: 2, y: 2, z: 4, core: 2. Of those that a mesh axis runs over, the one named last changes fastest.
Arguments:
- tokens: bfloat16 [80, 8192], P(('grp', 'blk'), 'bulk'), parts along dimension 0, may hold values from -6 to 6
- cotangent: bfloat16 [80, 8192], P(('grp', 'blk'), 'bulk'), parts along dimension 0, may hold values from -1.5 to 1.5
- gate_weight: bfloat16 [8192, 26624], P('bulk', 'blk'), may hold values from -0.0625 to 0.0625
- up_weight: bfloat16 [8192, 26624], P('bulk', 'blk'), may hold values from -0.0625 to 0.0625
- down_weight: bfloat16 [26624, 8192], P('blk', 'bulk'), may hold values from -0.0390625 to 0.0390625
Outputs:
- mixed: bfloat16 [80, 8192], P(('grp', 'blk'), 'bulk'), parts along dimension 0
- grad_input: bfloat16 [80, 8192], P(('grp', 'blk'), 'bulk'), parts along dimension 0
The draws below stay inside these ranges and needn't reach their ends.
There are 2 independent parts, one for each index of `grp`. The reference program is written for one: setup_inputs(seed, part) draws one part's arguments, and reference() takes and returns one part's arrays. A program takes and returns all parts, laid end to end along the dimension named above; an argument that names none is the same for every part. Nothing has to cross between parts.
All inputs are finite; a program needn't handle non-finite values.
Results may differ from the reference program's by a relative error of at most 0.0049.
Values may be sent and summed in bfloat16 or wider, within the bound.
A program may use at most 192 MiB of HBM per device.

```python
import jax
import jax.numpy as jnp
from jax import lax

D = 8192
FF = 26624
TOKENS = 40


def levels(rng, dims, split, low, largest):
    def one(position, shards_of):
        draws = jax.random.uniform(jax.random.fold_in(jax.random.fold_in(rng, 6), position), (shards_of,), jnp.float32, low / len(split), largest / len(split))
        return jnp.repeat(jnp.exp(draws), dims[position] // shards_of).reshape((-1,) + (1,) * (len(dims) - position - 1))

    loudness = one(*split[0])
    for cut in split[1:]:
        loudness = loudness * one(*cut)
    return loudness


def normal_values(stream_key, extent, scale, reach, cuts=(), dtype=jnp.bfloat16):
    gain = levels(stream_key, extent, cuts, -0.22, 0.18) if cuts else 1.0
    values = jax.random.normal(stream_key, extent, jnp.float32) * scale * gain
    return jnp.minimum(jnp.maximum(values, -reach), reach).astype(dtype)


def setup_inputs(seed: int = 0, part: int = 0) -> dict:
    seeds = jax.random.split(jax.random.key(seed), 6)
    own_keys = jax.random.split(jax.random.fold_in(seeds[5], part), 6)
    tokens = normal_values(own_keys[0], (TOKENS, D), 1.0, 6.0, ((0, 4), (1, 4)))
    cotangent = normal_values(own_keys[1], (TOKENS, D), 0.25, 1.5, ((0, 4), (1, 4)))
    gate_weight = normal_values(seeds[2], (D, FF), D ** -0.5, 0.0625, ((0, 4), (1, 4)))
    up_weight = normal_values(seeds[3], (D, FF), D ** -0.5, 0.0625, ((0, 4), (1, 4)))
    down_weight = normal_values(seeds[4], (FF, D), FF ** -0.5, 0.0390625, ((0, 4), (1, 4)))
    return {"tokens": tokens, "cotangent": cotangent, "gate_weight": gate_weight, "up_weight": up_weight, "down_weight": down_weight}


def reference(tokens, cotangent, gate_weight, up_weight, down_weight):
    gate = jnp.dot(tokens, gate_weight, preferred_element_type=jnp.float32)
    upward = jnp.dot(tokens, up_weight, preferred_element_type=jnp.float32)
    sigma = jax.nn.sigmoid(gate)
    hidden = (gate * sigma * upward).astype(jnp.bfloat16)
    mixed = jnp.dot(hidden, down_weight, preferred_element_type=jnp.float32).astype(jnp.bfloat16)
    back = lax.dot_general(cotangent, down_weight, (((1,), (1,)), ((), ())), preferred_element_type=jnp.float32)
    d_up = (back * gate * sigma).astype(jnp.bfloat16)
    d_gate = (back * upward * sigma * (1.0 + gate * (1.0 - sigma))).astype(jnp.bfloat16)
    first_part = lax.dot_general(d_gate, gate_weight, (((1,), (1,)), ((), ())), preferred_element_type=jnp.float32)
    second_part = lax.dot_general(d_up, up_weight, (((1,), (1,)), ((), ())), preferred_element_type=jnp.float32)
    grad_input = (first_part + second_part).astype(jnp.bfloat16)
    return mixed, grad_input
```

```python
import functools

import jax
import jax.numpy as jnp
from jax import lax
from jax.experimental import pallas as pl
from jax.experimental.pallas import tpu as pltpu
from jax.sharding import PartitionSpec as P

MESH = pl.DeviceIdType.MESH
BF = jnp.bfloat16
F32 = jnp.float32

S1 = 1
S2 = 3
S3 = 4
S4 = 7
S5 = 8
S6 = 11
AHEAD = 8
RING = 3
NT = (((1,), (1,)), ((), ()))


def kernel(nb, nu, n, fc, tok_in, cot_in, wg_hbm, wu_hbm, wd_hbm, mixed_out, grad_out,
           wg, wu, wd, tok_g, cot_g, tok, cot, part, pair, far, act, mixed, grad, stage, zbuf,
           g_sem, u_sem, d_sem, tk_send, tk_recv, p_send, p_recv, f_send, f_recv,
           a_send, a_recv, fw_send, z_send, z_recv):
    b_me = lax.axis_index("blk")
    u_me = lax.axis_index("bulk")
    x_me, k_me = u_me // 2, u_me % 2
    chips = nu // 2
    rows = tok_in.shape[0]
    dh = grad.shape[2]
    partner = x_me * 2 + (1 - k_me)

    def load_gu(c):
        cols = pl.ds(pl.multiple_of(c * fc, fc), fc)
        return (pltpu.make_async_copy(wg_hbm.at[:, cols], wg.at[c], g_sem.at[c]),
                pltpu.make_async_copy(wu_hbm.at[:, cols], wu.at[c], u_sem.at[c]))

    def load_d(m):
        c = m % n
        slot = m % RING
        return pltpu.make_async_copy(
            wd_hbm.at[pl.ds(pl.multiple_of(c * fc, fc), fc), :], wd.at[slot], d_sem.at[slot])

    ahead = min(AHEAD, n)
    for c in range(ahead):
        for cp in load_gu(c):
            cp.start()
        if c < RING:
            load_d(c).start()

    barrier = pltpu.get_barrier_semaphore()
    for d in range(1, nb):
        pl.semaphore_signal(barrier, inc=1, device_id={"blk": (b_me + d) % nb}, device_id_type=MESH)
    for d in range(1, nu):
        pl.semaphore_signal(barrier, inc=1, device_id={"bulk": (u_me + d) % nu}, device_id_type=MESH)
    pl.semaphore_wait(barrier, nb + nu - 2)

    def rcopy(src, dst, ss, rs, where):
        return pltpu.make_async_remote_copy(
            src_ref=src, dst_ref=dst, send_sem=ss, recv_sem=rs, device_id=where, device_id_type=MESH)

    def tok_copy(w, d):
        src, dst = (tok_in, tok_g) if w == 0 else (cot_in, cot_g)
        return rcopy(src, dst.at[d - 1], tk_send.at[w, d - 1], tk_recv.at[w, d - 1],
                     {"blk": (b_me + d) % nb})

    for w in range(2):
        for d in range(1, nb):
            tok_copy(w, d).start()
    for src, got, dst, which in ((tok_in, tok_g, tok, 0), (cot_in, cot_g, cot, 1)):
        for d in range(1, nb):
            tok_copy(which, d).wait_recv()
        for h in range(2):
            cols = pl.ds(h * dh, dh)
            for b in range(nb):
                slot = (b_me - b + nb) % nb
                other = got[jnp.maximum(slot - 1, 0), :, cols].astype(F32)
                own = src[:, cols].astype(F32)
                mixed[h, pl.ds(b * rows, rows), :] = jnp.where(slot == 0, own, other)
        for h in range(2):
            dst[:, h * dh:(h + 1) * dh] = mixed[h].astype(BF)

    def owner(c):
        o = c % nu
        return o, o // 2, o % 2

    def pair_copy(c):
        return rcopy(part.at[c], pair.at[c // 2], p_send.at[c], p_recv.at[c // 2], {"bulk": partner})

    def far_copy(c):
        o, ox, ok = owner(c)
        slot = (x_me - ox + chips - 1 + chips) % chips
        return rcopy(pair.at[c // 2], far.at[c // nu, slot], f_send.at[c // 2],
                     f_recv.at[c // nu, slot], {"bulk": o})

    def far_wait(c, slot):
        rcopy(pair.at[c // 2], far.at[c // nu, slot], f_send.at[c // 2],
              f_recv.at[c // nu, slot], {"bulk": partner}).wait_recv()

    def act_copy(c, d):
        to = partner if d == 0 else ((x_me + d) % chips) * 2 + k_me
        return rcopy(act.at[c], act.at[c], a_send.at[c // nu, d], a_recv.at[c], {"bulk": to})

    def forward(c):
        return rcopy(act.at[c], act.at[c], fw_send.at[c // 2], a_recv.at[c], {"bulk": partner})

    def valid(c):
        return jnp.logical_and(c >= 0, c < n)

    def stages(i):
        c1 = i - S1

        @pl.when(jnp.logical_and(valid(c1), owner(c1 + nu)[2] != k_me))
        def _():
            pair_copy(c1).start()

        c3 = i - S3
        o3 = owner(c3 + nu)

        @pl.when(jnp.logical_and(valid(c3), jnp.logical_and(o3[2] == k_me, o3[1] != x_me)))
        def _():
            far_copy(c3).start()

        c5 = i - S5

        @pl.when(jnp.logical_and(valid(c5), owner(c5 + nu)[0] == u_me))
        def _():
            for d in range(chips):
                act_copy(c5, d).start()

        c6 = i - S6
        o6 = owner(c6 + nu)

        @pl.when(jnp.logical_and(valid(c6), jnp.logical_and(o6[2] == k_me, o6[1] != x_me)))
        def _():
            forward(c6).wait_recv()
            forward(c6).start()

        c2 = i - S2
        o2 = owner(c2 + nu)

        @pl.when(jnp.logical_and(valid(c2), o2[2] == k_me))
        def _():
            pair_copy(c2).wait_recv()

            @pl.when(o2[1] != x_me)
            def _():
                for j in range(3):
                    pair[c2 // 2, j] = (
                        part[c2, j].astype(F32) + pair[c2 // 2, j].astype(F32)).astype(BF)

        c4 = i - S4

        @pl.when(jnp.logical_and(valid(c4), owner(c4 + nu)[0] == u_me))
        def _():
            for slot in range(chips - 1):
                far_wait(c4, slot)

            def total(j):
                s = part[c4, j].astype(F32) + pair[c4 // 2, j].astype(F32)
                for slot in range(chips - 1):
                    s = s + far[c4 // nu, slot, j].astype(F32)
                return s

            gate, upward, back = total(0), total(1), total(2)
            sigma = 1.0 / (1.0 + jnp.exp(-gate))
            act[c4, 0] = (gate * sigma * upward).astype(BF)
            act[c4, 1] = (back * upward * sigma * (1.0 + gate * (1.0 - sigma))).astype(BF)
            act[c4, 2] = (back * gate * sigma).astype(BF)

    def first(i, _):
        stages(i)

        @pl.when(i + ahead < n)
        def _():
            for cp in load_gu(i + ahead):
                cp.start()

        for cp in load_gu(i):
            cp.wait()
        part[i, 0] = jnp.dot(tok[...], wg[i], preferred_element_type=F32).astype(BF)
        part[i, 1] = jnp.dot(tok[...], wu[i], preferred_element_type=F32).astype(BF)
        load_d(i).wait()
        part[i, 2] = lax.dot_general(
            cot[...], wd[i % RING], NT, preferred_element_type=F32).astype(BF)
        load_d(i + RING).start()
        return 0

    lax.fori_loop(0, n, first, 0)

    mixed[...] = jnp.zeros_like(mixed)
    grad[...] = jnp.zeros_like(grad)

    def second(j, _):
        i = j + n
        stages(i)

        @pl.when(owner(j)[2] != k_me)
        def _():
            forward(j).wait_recv()

        load_d(i).wait()
        for h in range(2):
            mixed[h] += jnp.dot(
                act[j, 0], wd[i % RING, :, h * dh:(h + 1) * dh], preferred_element_type=F32)

        @pl.when(i + RING < 2 * n)
        def _():
            load_d(i + RING).start()

        return 0

    lax.fori_loop(0, n, second, 0)

    def z_stage(q):
        acc = mixed if q < 2 else grad
        for b in range(nb):
            stage[q, b] = acc[q % 2, b * rows:(b + 1) * rows, :].astype(BF)

    def z_copy(q, d):
        to = (b_me + d) % nb
        return rcopy(stage.at[q, to], zbuf.at[q, d - 1], z_send.at[q, d - 1], z_recv.at[q, d - 1],
                     {"blk": to})

    def z_send_all(q):
        for d in range(1, nb):
            z_copy(q, d).start()

    def z_finish(q):
        acc, out = (mixed, mixed_out) if q < 2 else (grad, grad_out)
        h = q % 2
        s = jnp.zeros((rows, dh), F32)
        for b in range(nb):
            s = s + jnp.where(b == b_me, acc[h, b * rows:(b + 1) * rows, :], 0.0)
        for d in range(1, nb):
            z_copy(q, d).wait_recv()
            s = s + zbuf[q, d - 1].astype(F32)
        out[:, h * dh:(h + 1) * dh] = s.astype(BF)

    z_stage(0)
    z_stage(1)
    for h in range(2):
        def third(c, _, h=h):
            @pl.when(c == 1)
            def _():
                for q in ((0, 1) if h == 0 else (2,)):
                    z_send_all(q)

            grad[h] += (
                lax.dot_general(act[c, 1], wg[c, h * dh:(h + 1) * dh, :], NT,
                                preferred_element_type=F32)
                + lax.dot_general(act[c, 2], wu[c, h * dh:(h + 1) * dh, :], NT,
                                  preferred_element_type=F32))
            return 0

        lax.fori_loop(0, n, third, 0)
        z_stage(2 + h)
    z_finish(0)
    z_send_all(3)
    z_finish(1)
    z_finish(2)

    for d in range(1, nb):
        for w in range(2):
            tok_copy(w, d).wait_send()

    def drain(c, _):
        o, ox, ok = owner(c)

        @pl.when(ok != k_me)
        def _():
            pair_copy(c).wait_send()

        @pl.when(jnp.logical_and(ok == k_me, ox != x_me))
        def _():
            far_copy(c).wait_send()
            forward(c).wait_send()

        @pl.when(o == u_me)
        def _():
            for d in range(chips):
                act_copy(c, d).wait_send()

        return 0

    lax.fori_loop(0, n, drain, 0)
    z_finish(3)
    for q in range(4):
        for d in range(1, nb):
            z_copy(q, d).wait_send()


def per_device(nb, nu, tokens, cotangent, gate_weight, up_weight, down_weight):
    rows, depth = tokens.shape
    width = gate_weight.shape[1]
    fc = next(w for w in (256, 128) if width % w == 0)
    n = width // fc
    assert n >= S6 and depth % 256 == 0 and nu % 2 == 0
    t = rows * nb
    dh = depth // 2
    owned = pl.cdiv(n, nu)
    halfn = pl.cdiv(n, 2)
    chips = nu // 2
    dma = pltpu.SemaphoreType.DMA
    vm = pltpu.VMEM
    out = jax.ShapeDtypeStruct((rows, depth), BF)
    return pl.pallas_call(
        functools.partial(kernel, nb, nu, n, fc),
        out_shape=(out, out),
        in_specs=[pl.BlockSpec(memory_space=pltpu.VMEM)] * 2 + [pl.BlockSpec(memory_space=pl.ANY)] * 3,
        out_specs=(pl.BlockSpec(memory_space=pltpu.VMEM),) * 2,
        scratch_shapes=[
            vm((n, depth, fc), BF), vm((n, depth, fc), BF), vm((RING, fc, depth), BF),
            vm((nb - 1, rows, depth), BF), vm((nb - 1, rows, depth), BF),
            vm((t, depth), BF), vm((t, depth), BF),
            vm((n, 3, t, fc), BF), vm((halfn, 3, t, fc), BF), vm((owned, chips - 1, 3, t, fc), BF),
            vm((n, 3, t, fc), BF),
            vm((2, t, dh), F32), vm((2, t, dh), F32),
            vm((4, nb, rows, dh), BF), vm((4, nb - 1, rows, dh), BF),
            dma((n,)), dma((n,)), dma((RING,)),
            dma((2, nb - 1)), dma((2, nb - 1)),
            dma((n,)), dma((halfn,)), dma((halfn,)), dma((owned, chips - 1)),
            dma((owned, chips)), dma((n,)), dma((halfn,)),
            dma((4, nb - 1)), dma((4, nb - 1)),
        ],
        compiler_params=pltpu.CompilerParams(
            collective_id=0, has_side_effects=True, vmem_limit_bytes=67043328),
    )(tokens, cotangent, gate_weight, up_weight, down_weight)


def solution(mesh):
    return jax.shard_map(
        functools.partial(per_device, mesh.shape["blk"], mesh.shape["bulk"]),
        mesh=mesh,
        in_specs=(
            P(("grp", "blk"), "bulk"),
            P(("grp", "blk"), "bulk"),
            P("bulk", "blk"),
            P("bulk", "blk"),
            P("blk", "bulk"),
        ),
        out_specs=(P(("grp", "blk"), "bulk"), P(("grp", "blk"), "bulk")),
        check_vma=False,
    )
```

```python
import functools

import jax
import jax.numpy as jnp
from jax import lax
from jax.experimental import pallas as pl
from jax.experimental.pallas import tpu as pltpu
from jax.sharding import PartitionSpec as P

MESH = pl.DeviceIdType.MESH
BF = jnp.bfloat16
F32 = jnp.float32

AHEAD = 12
RING = 3
LAG = 6
def lags(n):
    return (1, 3, 5, 9, 10, 15) if n >= 24 else (1, 3, 4, 7, 8, 11)


NT = (((1,), (1,)), ((), ()))


def kernel(nb, nu, n, fc, tok_in, cot_in, wg_hbm, wu_hbm, wd_hbm, out,
           wg, wu, wd, tok_g, cot_g, tok, cot, part, pair, chip, far, act, mixed, grad, stage, zbuf,
           g_sem, u_sem, d_sem, tk_send, tk_recv, p_send, p_recv, f_send, f_recv,
           a_send, a_recv, fw_send, z_send, z_recv):
    S1, S2, S3, S4, S5, S6 = lags(n)
    b_me = lax.axis_index("blk")
    u_me = lax.axis_index("bulk")
    x_me, k_me = u_me // 2, u_me % 2
    chips = nu // 2
    rows = tok_in.shape[0]
    dh = grad.shape[2]
    partner = x_me * 2 + (1 - k_me)

    def load_gu(c):
        cols = pl.ds(pl.multiple_of(c * fc, fc), fc)
        return (pltpu.make_async_copy(wg_hbm.at[:, cols], wg.at[c], g_sem.at[c]),
                pltpu.make_async_copy(wu_hbm.at[:, cols], wu.at[c], u_sem.at[c]))

    def load_d(m):
        m = jnp.int32(m)
        c = lax.rem(m, n)
        slot = lax.rem(m, RING)
        return pltpu.make_async_copy(
            wd_hbm.at[pl.ds(pl.multiple_of(c * fc, fc), fc), :], wd.at[slot], d_sem.at[slot])

    ahead = min(AHEAD, n)
    lag = min(LAG, n - S6)
    keep = part.shape[0]
    many = 2 if n % 2 == 0 else 1
    for c in range(ahead):
        for cp in load_gu(c):
            cp.start()
        if c < RING:
            load_d(c).start()

    barrier = pltpu.get_barrier_semaphore()
    for d in range(1, nb):
        pl.semaphore_signal(barrier, inc=1, device_id={"blk": (b_me + d) % nb}, device_id_type=MESH)
    for d in range(1, nu):
        pl.semaphore_signal(barrier, inc=1, device_id={"bulk": (u_me + d) % nu}, device_id_type=MESH)
    pl.semaphore_wait(barrier, nb + nu - 2)

    def rcopy(src, dst, ss, rs, where):
        return pltpu.make_async_remote_copy(
            src_ref=src, dst_ref=dst, send_sem=ss, recv_sem=rs, device_id=where, device_id_type=MESH)

    def tok_copy(w, d):
        src, dst = (tok_in, tok_g) if w == 0 else (cot_in, cot_g)
        return rcopy(src, dst.at[d - 1], tk_send.at[w, d - 1], tk_recv.at[w, d - 1],
                     {"blk": (b_me + d) % nb})

    for w in range(2):
        for d in range(1, nb):
            tok_copy(w, d).start()

    def gather(w):
        src, got, dst = (tok_in, tok_g, tok) if w == 0 else (cot_in, cot_g, cot)
        for d in range(1, nb):
            tok_copy(w, d).wait_recv()
        for h in range(2):
            cols = pl.ds(h * dh, dh)
            for b in range(nb):
                slot = (b_me - b + nb) % nb
                other = got[jnp.maximum(slot - 1, 0), :, cols].astype(F32)
                own = src[:, cols].astype(F32)
                mixed[h, pl.ds(b * rows, rows), :] = jnp.where(slot == 0, own, other)
        for h in range(2):
            dst[:, h * dh:(h + 1) * dh] = mixed[h].astype(BF)

    def owner(c):
        o = lax.rem(c, nu)
        return o, lax.div(o, 2), lax.rem(o, 2)

    def pair_copy(c):
        return rcopy(part.at[lax.rem(c, keep)], pair.at[lax.div(c, 2)], p_send.at[c], p_recv.at[lax.div(c, 2)], {"bulk": partner})

    def far_copy(c):
        o, ox, ok = owner(c)
        slot = (x_me - ox + chips - 1 + chips) % chips
        return rcopy(chip.at[lax.div(c, 2)], far.at[lax.div(c, nu), slot], f_send.at[lax.div(c, 2)],
                     f_recv.at[lax.div(c, nu), slot], {"bulk": o})

    def far_wait(c, slot):
        rcopy(chip.at[lax.div(c, 2)], far.at[lax.div(c, nu), slot], f_send.at[lax.div(c, 2)],
              f_recv.at[lax.div(c, nu), slot], {"bulk": partner}).wait_recv()

    def act_copy(c, d):
        to = partner if d == 0 else ((x_me + d) % chips) * 2 + k_me
        return rcopy(act.at[c], act.at[c], a_send.at[lax.div(c, nu), d], a_recv.at[c], {"bulk": to})

    def forward(c):
        return rcopy(act.at[c], act.at[c], fw_send.at[lax.div(c, 2)], a_recv.at[c], {"bulk": partner})

    def valid(c):
        return jnp.logical_and(c >= 0, c < n)

    def stages(i):
        c1 = i - S1

        @pl.when(jnp.logical_and(valid(c1), owner(c1 + nu)[2] != k_me))
        def _():
            pair_copy(c1).start()

        c3 = i - S3
        o3 = owner(c3 + nu)

        @pl.when(jnp.logical_and(valid(c3), jnp.logical_and(o3[2] == k_me, o3[1] != x_me)))
        def _():
            far_copy(c3).start()

        c5 = i - S5

        @pl.when(jnp.logical_and(valid(c5), owner(c5 + nu)[0] == u_me))
        def _():
            for d in range(chips):
                act_copy(c5, d).start()

        c6 = i - S6
        o6 = owner(c6 + nu)

        @pl.when(jnp.logical_and(valid(c6), jnp.logical_and(o6[2] == k_me, o6[1] != x_me)))
        def _():
            forward(c6).wait_recv()
            forward(c6).start()

        c2 = i - S2
        o2 = owner(c2 + nu)

        @pl.when(jnp.logical_and(valid(c2), o2[2] == k_me))
        def _():
            pair_copy(c2).wait_recv()

            @pl.when(o2[1] != x_me)
            def _():
                for j in range(3):
                    chip[lax.div(c2, 2), j] = (
                        part[lax.rem(c2, keep), j] + pair[lax.div(c2, 2), j]).astype(BF)

        c4 = i - S4

        @pl.when(jnp.logical_and(valid(c4), owner(c4 + nu)[2] != k_me))
        def _():
            pair_copy(c4).wait_send()

        @pl.when(jnp.logical_and(valid(c4), owner(c4 + nu)[0] == u_me))
        def _():
            for slot in range(chips - 1):
                far_wait(c4, slot)

            def total(j):
                s = part[lax.rem(c4, keep), j] + pair[lax.div(c4, 2), j]
                for slot in range(chips - 1):
                    s = s + far[lax.div(c4, nu), slot, j].astype(F32)
                return s

            gate, upward, back = total(0), total(1), total(2)
            sigma = 1.0 / (1.0 + jnp.exp(-gate))
            act[c4, 0] = (gate * sigma * upward).astype(BF)
            act[c4, 1] = (back * upward * sigma * (1.0 + gate * (1.0 - sigma))).astype(BF)
            act[c4, 2] = (back * gate * sigma).astype(BF)

    def first(gu, back, i, _):
        m = i - lag
        stages(m)
        if gu:
            @pl.when(i + ahead < n)
            def _():
                for cp in load_gu(i + ahead):
                    cp.start()

            for cp in load_gu(i):
                cp.wait()
        if back:
            load_d(m).wait()
        if gu:
            part[lax.rem(i, keep), 0] = jnp.dot(tok[...], wg[i], preferred_element_type=F32)
            part[lax.rem(i, keep), 1] = jnp.dot(tok[...], wu[i], preferred_element_type=F32)
        if back:
            part[lax.rem(m, keep), 2] = lax.dot_general(
                cot[...], wd[lax.rem(m, RING)], NT, preferred_element_type=F32)
            load_d(m + RING).start()
        return 0

    gather(0)
    lax.fori_loop(0, lag, functools.partial(first, True, False), 0)
    gather(1)
    lax.fori_loop(lag, n, functools.partial(first, True, True), 0)
    lax.fori_loop(n, n + lag, functools.partial(first, False, True), 0)

    mixed[...] = jnp.zeros_like(mixed)
    grad[...] = jnp.zeros_like(grad)

    def add_grad(h, c):
        grad[h] += (
            lax.dot_general(act[c, 1], wg[c, h * dh:(h + 1) * dh, :], NT,
                            preferred_element_type=F32)
            + lax.dot_general(act[c, 2], wu[c, h * dh:(h + 1) * dh, :], NT,
                              preferred_element_type=F32))

    def second(j, _):
        m = j + n
        stages(m)

        @pl.when(owner(j)[2] != k_me)
        def _():
            forward(j).wait_recv()

        load_d(m).wait()
        add_grad(0, j)
        for h in range(2):
            mixed[h] += jnp.dot(
                act[j, 0], wd[lax.rem(m, RING), :, h * dh:(h + 1) * dh], preferred_element_type=F32)

        @pl.when(m + RING < 2 * n)
        def _():
            load_d(m + RING).start()

        return 0

    lax.fori_loop(0, n, second, 0)

    def z_stage(q):
        acc = mixed if q < 2 else grad
        for b in range(nb):
            stage[q, b] = acc[q % 2, b * rows:(b + 1) * rows, :].astype(BF)

    def z_copy(q, d):
        to = (b_me + d) % nb
        return rcopy(stage.at[q, to], zbuf.at[q, d - 1], z_send.at[q, d - 1], z_recv.at[q, d - 1],
                     {"blk": to})

    def z_send_all(q):
        for d in range(1, nb):
            z_copy(q, d).start()

    def z_finish(q):
        acc = mixed if q < 2 else grad
        h = q % 2
        s = jnp.zeros((rows, dh), F32)
        for b in range(nb):
            s = s + jnp.where(b == b_me, acc[h, b * rows:(b + 1) * rows, :], 0.0)
        for d in range(1, nb):
            z_copy(q, d).wait_recv()
            s = s + zbuf[q, d - 1].astype(F32)
        out[q // 2, :, h * dh:(h + 1) * dh] = s

    for q in range(3):
        z_stage(q)

    def third(c, _):
        @pl.when(c == 1)
        def _():
            for q in range(3):
                z_send_all(q)

        for k in range(many):
            add_grad(1, c * many + k)
        return 0

    lax.fori_loop(0, n // many, third, 0)
    z_stage(3)
    z_finish(0)
    z_send_all(3)
    z_finish(1)
    z_finish(2)

    for d in range(1, nb):
        for w in range(2):
            tok_copy(w, d).wait_send()

    def drain(c, _):
        o, ox, ok = owner(c)

        @pl.when(jnp.logical_and(ok == k_me, ox != x_me))
        def _():
            far_copy(c).wait_send()
            forward(c).wait_send()

        @pl.when(o == u_me)
        def _():
            for d in range(chips):
                act_copy(c, d).wait_send()

        return 0

    lax.fori_loop(0, n, drain, 0)
    z_finish(3)
    for q in range(4):
        for d in range(1, nb):
            z_copy(q, d).wait_send()


def per_device(nb, nu, tokens, cotangent, gate_weight, up_weight, down_weight):
    rows, depth = tokens.shape
    width = gate_weight.shape[1]
    fc = next(w for w in (256, 128) if width % w == 0)
    n = width // fc
    S4, S6 = lags(n)[3], lags(n)[5]
    assert n >= S6 and depth % 256 == 0 and nu % 2 == 0
    t = rows * nb
    dh = depth // 2
    owned = pl.cdiv(n, nu)
    halfn = pl.cdiv(n, 2)
    chips = nu // 2
    dma = pltpu.SemaphoreType.DMA
    vm = pltpu.VMEM
    both = pl.pallas_call(
        functools.partial(kernel, nb, nu, n, fc),
        out_shape=jax.ShapeDtypeStruct((2, rows, depth), F32),
        in_specs=[pl.BlockSpec(memory_space=pltpu.VMEM)] * 2 + [pl.BlockSpec(memory_space=pl.ANY)] * 3,
        out_specs=pl.BlockSpec(memory_space=pltpu.VMEM),
        scratch_shapes=[
            vm((n, depth, fc), BF), vm((n, depth, fc), BF), vm((RING, fc, depth), BF),
            vm((nb - 1, rows, depth), BF), vm((nb - 1, rows, depth), BF),
            vm((t, depth), BF), vm((t, depth), BF),
            vm((S4 + min(LAG, n - S6), 3, t, fc), F32), vm((halfn, 3, t, fc), F32), vm((halfn, 3, t, fc), BF), vm((owned, chips - 1, 3, t, fc), BF),
            vm((n, 3, t, fc), BF),
            vm((2, t, dh), F32), vm((2, t, dh), F32),
            vm((4, nb, rows, dh), BF), vm((4, nb - 1, rows, dh), BF),
            dma((n,)), dma((n,)), dma((RING,)),
            dma((2, nb - 1)), dma((2, nb - 1)),
            dma((n,)), dma((halfn,)), dma((halfn,)), dma((owned, chips - 1)),
            dma((owned, chips)), dma((n,)), dma((halfn,)),
            dma((4, nb - 1)), dma((4, nb - 1)),
        ],
        compiler_params=pltpu.CompilerParams(
            collective_id=0, has_side_effects=True, vmem_limit_bytes=67043328),
    )(tokens, cotangent, gate_weight, up_weight, down_weight)
    return both[0].astype(BF), both[1].astype(BF)


def solution(mesh):
    return jax.shard_map(
        functools.partial(per_device, mesh.shape["blk"], mesh.shape["bulk"]),
        mesh=mesh,
        in_specs=(
            P(("grp", "blk"), "bulk"),
            P(("grp", "blk"), "bulk"),
            P("bulk", "blk"),
            P("bulk", "blk"),
            P("blk", "bulk"),
        ),
        out_specs=(P(("grp", "blk"), "bulk"), P(("grp", "blk"), "bulk")),
        check_vma=False,
    )
```

```python
import functools

import jax
import jax.numpy as jnp
from jax import lax
from jax.experimental import pallas as pl
from jax.experimental.pallas import tpu as pltpu
from jax.sharding import PartitionSpec as P

MESH = pl.DeviceIdType.MESH
BF = jnp.bfloat16
F32 = jnp.float32

AHEAD = 20
RING = 3
LAG = 4
def lags(n):
    return (1, 3, 5, 9, 10, 15) if n >= 24 else (1, 3, 4, 7, 8, 11)


NT = (((1,), (1,)), ((), ()))


def kernel(nb, nu, n, fc, tok_in, cot_in, wg_hbm, wu_hbm, wd_hbm, out,
           wg, wu, wd, own, tok_g, cot_g, tok, cot, part, pair, chip, far, act, mixed, grad, stage, zbuf,
           g_sem, u_sem, d_sem, tk_send, tk_recv, p_send, p_recv, f_send, f_recv,
           a_send, a_recv, fw_send, z_send, z_recv):
    S1, S2, S3, S4, S5, S6 = lags(n)
    b_me = lax.axis_index("blk")
    u_me = lax.axis_index("bulk")
    x_me, k_me = u_me // 2, u_me % 2
    chips = nu // 2
    rows = tok_in.shape[0]
    dh = grad.shape[2]
    partner = x_me * 2 + (1 - k_me)

    def load_gu(c):
        cols = pl.ds(pl.multiple_of(c * fc, fc), fc)
        return (pltpu.make_async_copy(wg_hbm.at[:, cols], wg.at[c], g_sem.at[c]),
                pltpu.make_async_copy(wu_hbm.at[:, cols], wu.at[c], u_sem.at[c]))

    def load_d(m):
        m = jnp.int32(m)
        c = lax.rem(m, n)
        slot = lax.rem(m, RING)
        return pltpu.make_async_copy(
            wd_hbm.at[pl.ds(pl.multiple_of(c * fc, fc), fc), :], wd.at[slot], d_sem.at[slot])

    ahead = min(AHEAD, n)
    lag = min(LAG, n - S6)
    keep = part.shape[0]
    many = 2 if n % 2 == 0 else 1
    for c in range(ahead):
        for cp in load_gu(c):
            cp.start()
        if c < RING:
            load_d(c).start()

    own[...] = jnp.zeros_like(own)
    own[0, :rows, :] = tok_in[...]
    own[1, :rows, :] = cot_in[...]
    stage[...] = jnp.zeros_like(stage)

    barrier = pltpu.get_barrier_semaphore()
    for d in range(1, nb):
        pl.semaphore_signal(barrier, inc=1, device_id={"blk": (b_me + d) % nb}, device_id_type=MESH)
    for d in range(1, nu):
        pl.semaphore_signal(barrier, inc=1, device_id={"bulk": (u_me + d) % nu}, device_id_type=MESH)
    pl.semaphore_wait(barrier, nb + nu - 2)

    def rcopy(src, dst, ss, rs, where):
        return pltpu.make_async_remote_copy(
            src_ref=src, dst_ref=dst, send_sem=ss, recv_sem=rs, device_id=where, device_id_type=MESH)

    def tok_copy(w, d):
        dst = tok_g if w == 0 else cot_g
        return rcopy(own.at[w], dst.at[d - 1], tk_send.at[w, d - 1], tk_recv.at[w, d - 1],
                     {"blk": (b_me + d) % nb})

    for w in range(2):
        for d in range(1, nb):
            tok_copy(w, d).start()

    def gather(w):
        src, got, dst = (tok_in, tok_g, tok) if w == 0 else (cot_in, cot_g, cot)
        for d in range(1, nb):
            tok_copy(w, d).wait_recv()
        for h in range(2):
            cols = pl.ds(h * dh, dh)
            for b in range(nb):
                slot = (b_me - b + nb) % nb
                other = got[jnp.maximum(slot - 1, 0), :rows, cols].astype(F32)
                mine = src[:, cols].astype(F32)
                mixed[h, pl.ds(b * rows, rows), :] = jnp.where(slot == 0, mine, other)
        for h in range(2):
            dst[:, h * dh:(h + 1) * dh] = mixed[h].astype(BF)

    def owner(c):
        o = lax.rem(c, nu)
        return o, lax.div(o, 2), lax.rem(o, 2)

    def pair_copy(c):
        return rcopy(part.at[lax.rem(c, keep)], pair.at[lax.div(c, 2)], p_send.at[c], p_recv.at[lax.div(c, 2)], {"bulk": partner})

    def far_copy(c):
        o, ox, ok = owner(c)
        slot = (x_me - ox + chips - 1 + chips) % chips
        return rcopy(chip.at[lax.div(c, 2)], far.at[lax.div(c, nu), slot], f_send.at[lax.div(c, 2)],
                     f_recv.at[lax.div(c, nu), slot], {"bulk": o})

    def far_wait(c, slot):
        rcopy(chip.at[lax.div(c, 2)], far.at[lax.div(c, nu), slot], f_send.at[lax.div(c, 2)],
              f_recv.at[lax.div(c, nu), slot], {"bulk": partner}).wait_recv()

    def act_copy(c, d):
        to = partner if d == 0 else ((x_me + d) % chips) * 2 + k_me
        return rcopy(act.at[c], act.at[c], a_send.at[lax.div(c, nu), d], a_recv.at[c], {"bulk": to})

    def forward(c):
        return rcopy(act.at[c], act.at[c], fw_send.at[lax.div(c, 2)], a_recv.at[c], {"bulk": partner})

    def valid(c):
        return jnp.logical_and(c >= 0, c < n)

    def stages(i):
        c1 = i - S1

        @pl.when(jnp.logical_and(valid(c1), owner(c1 + nu)[2] != k_me))
        def _():
            pair_copy(c1).start()

        c3 = i - S3
        o3 = owner(c3 + nu)

        @pl.when(jnp.logical_and(valid(c3), jnp.logical_and(o3[2] == k_me, o3[1] != x_me)))
        def _():
            far_copy(c3).start()

        c5 = i - S5

        @pl.when(jnp.logical_and(valid(c5), owner(c5 + nu)[0] == u_me))
        def _():
            for d in range(chips):
                act_copy(c5, d).start()

        c6 = i - S6
        o6 = owner(c6 + nu)

        @pl.when(jnp.logical_and(valid(c6), jnp.logical_and(o6[2] == k_me, o6[1] != x_me)))
        def _():
            forward(c6).wait_recv()
            forward(c6).start()

        c2 = i - S2
        o2 = owner(c2 + nu)

        @pl.when(jnp.logical_and(valid(c2), o2[2] == k_me))
        def _():
            pair_copy(c2).wait_recv()

            @pl.when(o2[1] != x_me)
            def _():
                for j in range(3):
                    chip[lax.div(c2, 2), j] = (
                        part[lax.rem(c2, keep), j] + pair[lax.div(c2, 2), j]).astype(BF)

        c4 = i - S4

        @pl.when(jnp.logical_and(valid(c4), owner(c4 + nu)[2] != k_me))
        def _():
            pair_copy(c4).wait_send()

        @pl.when(jnp.logical_and(valid(c4), owner(c4 + nu)[0] == u_me))
        def _():
            for slot in range(chips - 1):
                far_wait(c4, slot)

            def total(j):
                s = part[lax.rem(c4, keep), j] + pair[lax.div(c4, 2), j]
                for slot in range(chips - 1):
                    s = s + far[lax.div(c4, nu), slot, j].astype(F32)
                return s

            gate, upward, back = total(0), total(1), total(2)
            sigma = 1.0 / (1.0 + jnp.exp(-gate))
            act[c4, 0] = (gate * sigma * upward).astype(BF)
            act[c4, 1] = (back * upward * sigma * (1.0 + gate * (1.0 - sigma))).astype(BF)
            act[c4, 2] = (back * gate * sigma).astype(BF)

    def first(gu, back, i, _):
        m = i - lag
        stages(m)
        if gu:
            @pl.when(i + ahead < n)
            def _():
                for cp in load_gu(i + ahead):
                    cp.start()

            for cp in load_gu(i):
                cp.wait()
        if back:
            load_d(m).wait()
        if gu:
            part[lax.rem(i, keep), 0] = jnp.dot(tok[...], wg[i], preferred_element_type=F32)
            part[lax.rem(i, keep), 1] = jnp.dot(tok[...], wu[i], preferred_element_type=F32)
        if back:
            part[lax.rem(m, keep), 2] = lax.dot_general(
                cot[...], wd[lax.rem(m, RING)], NT, preferred_element_type=F32)
            load_d(m + RING).start()
        return 0

    gather(0)
    lax.fori_loop(0, lag, functools.partial(first, True, False), 0)
    gather(1)
    lax.fori_loop(lag, n, functools.partial(first, True, True), 0)
    lax.fori_loop(n, n + lag, functools.partial(first, False, True), 0)

    mixed[...] = jnp.zeros_like(mixed)
    grad[...] = jnp.zeros_like(grad)

    def add_grad(h, c):
        grad[h] += (
            lax.dot_general(act[c, 1], wg[c, h * dh:(h + 1) * dh, :], NT,
                            preferred_element_type=F32)
            + lax.dot_general(act[c, 2], wu[c, h * dh:(h + 1) * dh, :], NT,
                              preferred_element_type=F32))

    def second(j, _):
        m = j + n
        stages(m)

        @pl.when(owner(j)[2] != k_me)
        def _():
            forward(j).wait_recv()

        load_d(m).wait()
        add_grad(0, j)
        for h in range(2):
            mixed[h] += jnp.dot(
                act[j, 0], wd[lax.rem(m, RING), :, h * dh:(h + 1) * dh], preferred_element_type=F32)

        @pl.when(m + RING < 2 * n)
        def _():
            load_d(m + RING).start()

        return 0

    lax.fori_loop(0, n, second, 0)

    def z_stage(q):
        acc = mixed if q < 2 else grad
        for b in range(nb):
            stage[q, b, :rows, :] = acc[q % 2, b * rows:(b + 1) * rows, :].astype(BF)

    def z_copy(q, d):
        to = (b_me + d) % nb
        return rcopy(stage.at[q, to], zbuf.at[q, d - 1], z_send.at[q, d - 1], z_recv.at[q, d - 1],
                     {"blk": to})

    def z_send_all(q):
        for d in range(1, nb):
            z_copy(q, d).start()

    def z_finish(q):
        acc = mixed if q < 2 else grad
        h = q % 2
        s = jnp.zeros((rows, dh), F32)
        for b in range(nb):
            s = s + jnp.where(b == b_me, acc[h, b * rows:(b + 1) * rows, :], 0.0)
        for d in range(1, nb):
            z_copy(q, d).wait_recv()
            s = s + zbuf[q, d - 1, :rows, :].astype(F32)
        out[q // 2, :, h * dh:(h + 1) * dh] = s

    for q in range(3):
        z_stage(q)

    def third(c, _):
        @pl.when(c == 1)
        def _():
            for q in range(3):
                z_send_all(q)

        for k in range(many):
            add_grad(1, c * many + k)
        return 0

    lax.fori_loop(0, n // many, third, 0)
    z_stage(3)
    z_finish(0)
    z_send_all(3)
    z_finish(1)
    z_finish(2)

    for d in range(1, nb):
        for w in range(2):
            tok_copy(w, d).wait_send()

    def drain(c, _):
        o, ox, ok = owner(c)

        @pl.when(jnp.logical_and(ok == k_me, ox != x_me))
        def _():
            far_copy(c).wait_send()
            forward(c).wait_send()

        @pl.when(o == u_me)
        def _():
            for d in range(chips):
                act_copy(c, d).wait_send()

        return 0

    lax.fori_loop(0, n, drain, 0)
    z_finish(3)
    for q in range(4):
        for d in range(1, nb):
            z_copy(q, d).wait_send()


def per_device(nb, nu, tokens, cotangent, gate_weight, up_weight, down_weight):
    rows, depth = tokens.shape
    width = gate_weight.shape[1]
    fc = next(w for w in (256, 128) if width % w == 0)
    n = width // fc
    S4, S6 = lags(n)[3], lags(n)[5]
    assert n >= S6 and depth % 256 == 0 and nu % 2 == 0
    t = rows * nb
    tile = pl.cdiv(rows, 16) * 16
    dh = depth // 2
    owned = pl.cdiv(n, nu)
    halfn = pl.cdiv(n, 2)
    chips = nu // 2
    dma = pltpu.SemaphoreType.DMA
    vm = pltpu.VMEM
    both = pl.pallas_call(
        functools.partial(kernel, nb, nu, n, fc),
        out_shape=jax.ShapeDtypeStruct((2, rows, depth), F32),
        in_specs=[pl.BlockSpec(memory_space=pltpu.VMEM)] * 2 + [pl.BlockSpec(memory_space=pl.ANY)] * 3,
        out_specs=pl.BlockSpec(memory_space=pltpu.VMEM),
        scratch_shapes=[
            vm((n, depth, fc), BF), vm((n, depth, fc), BF), vm((RING, fc, depth), BF),
            vm((2, tile, depth), BF), vm((nb - 1, tile, depth), BF), vm((nb - 1, tile, depth), BF),
            vm((t, depth), BF), vm((t, depth), BF),
            vm((S4 + min(LAG, n - S6), 3, t, fc), F32), vm((halfn, 3, t, fc), F32), vm((halfn, 3, t, fc), BF), vm((owned, chips - 1, 3, t, fc), BF),
            vm((n, 3, t, fc), BF),
            vm((2, t, dh), F32), vm((2, t, dh), F32),
            vm((4, nb, tile, dh), BF), vm((4, nb - 1, tile, dh), BF),
            dma((n,)), dma((n,)), dma((RING,)),
            dma((2, nb - 1)), dma((2, nb - 1)),
            dma((n,)), dma((halfn,)), dma((halfn,)), dma((owned, chips - 1)),
            dma((owned, chips)), dma((n,)), dma((halfn,)),
            dma((4, nb - 1)), dma((4, nb - 1)),
        ],
        compiler_params=pltpu.CompilerParams(
            collective_id=0, has_side_effects=True, vmem_limit_bytes=67043328),
    )(tokens, cotangent, gate_weight, up_weight, down_weight)
    return both[0].astype(BF), both[1].astype(BF)


def solution(mesh):
    return jax.shard_map(
        functools.partial(per_device, mesh.shape["blk"], mesh.shape["bulk"]),
        mesh=mesh,
        in_specs=(
            P(("grp", "blk"), "bulk"),
            P(("grp", "blk"), "bulk"),
            P("bulk", "blk"),
            P("bulk", "blk"),
            P("blk", "bulk"),
        ),
        out_specs=(P(("grp", "blk"), "bulk"), P(("grp", "blk"), "bulk")),
        check_vma=False,
    )
```
